32 devices in a mesh: dom: 8 (over z, y), sub: 4 (over x, core).
Axes of the slice: x: 2, y: 2, z: 4, core: 2. Of those that a mesh axis runs over, the one named last changes fastest.
Arguments:
- nodal_values: float32 [512, 8192], P(None, ('dom', 'sub')), may hold values from -6 to 6
- kappa: float32 [512, 8192], P(None, ('dom', 'sub')), may hold values from 0.25 to 4
- levels: int32 [8192], P(('dom', 'sub')), may hold values from 0 to 3
- local_faces: int32 [2, 2048], P(None, ('dom', 'sub')), may hold values from 0 to 511, as said below
- sub_faces: int32 [2, 1024], P(None, ('dom', 'sub')), may hold values from 0 to 511, as said below
- near_faces: int32 [2, 1024], P(None, ('dom', 'sub')), may hold values from 512 to 1023, as said below
- far_faces: int32 [2, 384], P(None, ('dom', 'sub')), may hold values from 1024 to 1535, as said below
- child_faces: int32 [4, 96], P(None, ('dom', 'sub')), may hold values from 1024 to 1279, as said below
- child_peer: int32 [96], P(('dom', 'sub')), may hold values from 0 to 7, as said below
- coarse_faces: int32 [256], P(('dom', 'sub')), may hold values from -1 to 1535, as said below
Outputs:
- applied: float32 [512, 8192], P(None, ('dom', 'sub'))
The draws below stay inside these ranges and needn't reach their ends.
Inputs may be any that keep to these rules, and one draw needn't show every extreme that they name: `local_faces`: row 0 holds faces f = 1 and row 1 faces f = 0 of distinct elements of the same device; column k of both rows is one shared face. `sub_faces`: row 0 holds faces f = 0, row 1 faces f = 1, of distinct elements; entries toward a missing neighbour are boundary faces. `near_faces`: row 0 holds faces f = 2, row 1 faces f = 3, of distinct elements; entries toward a missing neighbour are boundary faces. `far_faces`: row 0 holds faces f = 4, row 1 faces f = 5, of distinct elements; entries toward a missing partner are boundary faces. `child_faces`: faces f = 4 of distinct elements, distinct from all far faces; row m is the child at subface position (m // 2, m % 2). `child_peer`: A device's 3 groups name distinct dom indices other than its own; in every draw one device per sub index is named by every other dom index. `coarse_faces`: slot p is the face f = 5 that takes the group which the device of dom index p (same sub index) sends here, -1 where it sends none; faces are of distinct elements, distinct from all far faces.
All inputs are finite; a program needn't handle non-finite values.
Results may differ from the reference program's by a relative error of at most 0.0003.
Values sent between devices are 32-bit elements; how exact they have to be, the bound alone decides.
A program may use at most 64 MiB of HBM per device.

```python
import math
import jax
import jax.numpy as jnp
import numpy as np
from jax import lax

NPTS = 8
E_DEV = 256
S_FACES = 32
NEAR = 32
L_PAIRS = 64
FAR = 4
SHIFTS = 3
NODES = 512
ELEMS = 8192
N_DOM = 8
N_SUB = 4


def element_orders(key):
    devices = N_DOM * N_SUB
    keys = jax.random.split(jax.random.fold_in(key, 11), 3 * devices)
    orders = jax.vmap(lambda item: jax.random.permutation(item, E_DEV))(keys)
    return orders.reshape(3, devices, E_DEV).astype(jnp.int32)


def mortar_plan(key):
    count = 3 * N_DOM // 8
    hub = jax.random.randint(jax.random.fold_in(key, 31), (N_SUB,), 0, N_DOM)
    keys = jax.random.split(jax.random.fold_in(key, 37), N_DOM * N_SUB)
    ranks = jax.vmap(lambda item: jax.random.permutation(item, N_DOM))(keys).astype(jnp.int32)
    ranks = ranks.reshape(N_DOM, N_SUB, N_DOM)
    lanes = lax.iota(jnp.int32, N_DOM)
    scores = jnp.where(lanes[None, None, :] == hub[None, :, None], -1, ranks)
    scores = jnp.where(lanes[None, None, :] == lanes[:, None, None], N_DOM + 1, scores)
    chosen = jnp.argsort(scores, axis=-1, stable=True)[:, :, :count].astype(jnp.int32)
    shuffle_keys = jax.random.split(jax.random.fold_in(key, 41), N_DOM * N_SUB)
    shuffle = jax.vmap(lambda item: jax.random.permutation(item, count))(shuffle_keys).astype(jnp.int32)
    return jnp.take_along_axis(chosen, shuffle.reshape(N_DOM, N_SUB, count), axis=-1)


def draw_local_faces(key, part):
    orders = element_orders(key)[0]
    first = E_DEV + orders[:, 2 * S_FACES:2 * S_FACES + L_PAIRS]
    second = orders[:, 2 * S_FACES + L_PAIRS:2 * S_FACES + 2 * L_PAIRS]
    return jnp.stack([first.reshape(-1), second.reshape(-1)]).astype(jnp.int32)


def draw_sub_faces(key, part):
    orders = element_orders(key)[0]
    lower = orders[:, :S_FACES]
    upper = E_DEV + orders[:, S_FACES:2 * S_FACES]
    return jnp.stack([lower.reshape(-1), upper.reshape(-1)]).astype(jnp.int32)


def draw_near_faces(key, part):
    orders = element_orders(key)[1]
    lower = 2 * E_DEV + orders[:, :NEAR]
    upper = 3 * E_DEV + orders[:, NEAR:2 * NEAR]
    return jnp.stack([lower.reshape(-1), upper.reshape(-1)]).astype(jnp.int32)


def draw_far_faces(key, part):
    span = SHIFTS * FAR
    orders = element_orders(key)[2]
    lower = 4 * E_DEV + orders[:, :span]
    upper = 5 * E_DEV + orders[:, span:2 * span]
    return jnp.stack([lower.reshape(-1), upper.reshape(-1)]).astype(jnp.int32)


def draw_child_faces(key, part):
    count = 3 * N_DOM // 8
    base = 2 * SHIFTS * FAR
    orders = element_orders(key)[2].reshape(N_DOM, N_SUB, E_DEV)
    elements = orders[:, :, base:base + 4 * count].reshape(N_DOM, N_SUB, count, 4)
    faces = 4 * E_DEV + elements
    return faces.transpose(3, 0, 1, 2).reshape(4, -1).astype(jnp.int32)


def draw_child_peer(key, part):
    return mortar_plan(key).reshape(-1).astype(jnp.int32)


def draw_coarse_faces(key, part):
    base = 2 * SHIFTS * FAR
    plan = mortar_plan(key)
    lanes = lax.iota(jnp.int32, N_DOM)
    sends = (plan[:, :, :, None] == lanes[None, None, None, :]).any(axis=2)
    receive = sends.transpose(2, 1, 0)
    rank = jnp.cumsum(receive.astype(jnp.int32), axis=2) - 1
    orders = element_orders(key)[2].reshape(N_DOM, N_SUB, E_DEV)
    elements = jnp.take_along_axis(orders, base + jnp.maximum(rank, 0), axis=2)
    faces = jnp.where(receive, 5 * E_DEV + elements, -1)
    return faces.reshape(-1).astype(jnp.int32)


def with_ends(drawn, stream_key, least, top_value):
    longest = drawn.shape.index(max(drawn.shape))
    spots = []
    for shift in (0, 1):
        where = [jax.random.randint(jax.random.fold_in(stream_key, axis), (), 0, length) for axis, length in enumerate(drawn.shape)]
        where[longest] = (where[longest] + shift) % drawn.shape[longest]
        spots.append(tuple(where))
    return drawn.at[spots[0]].set(least).at[spots[1]].set(top_value)


def level_of(key, dims, cuts, least, largest):
    def one(dim, blocks):
        draws = jax.random.uniform(jax.random.fold_in(jax.random.fold_in(key, 6), dim), (blocks,), jnp.float32, least / len(cuts), largest / len(cuts))
        return jnp.repeat(jnp.exp(draws), dims[dim] // blocks).reshape((-1,) + (1,) * (len(dims) - dim - 1))

    level = one(*cuts[0])
    for cut in cuts[1:]:
        level = level * one(*cut)
    return level


def centred(own_key, shape, scale, reach, cuts=(), kind=jnp.bfloat16):
    loudness = level_of(own_key, shape, cuts, -0.22, 0.18) if cuts else 1.0
    values = jax.random.normal(own_key, shape, jnp.float32) * scale * loudness
    return jnp.minimum(jnp.maximum(values, -reach), reach).astype(kind)


def setup_inputs(seed: int = 0) -> dict:
    key_list = jax.random.split(jax.random.key(seed), 11)
    nodal_values = centred(key_list[0], (NODES, ELEMS), 1.0, 6.0, ((1, 32),), jnp.float32)
    kappa = jnp.clip(jnp.exp(math.log(4.0) - 2.7725887 * jax.random.uniform(key_list[1], (NODES, ELEMS), jnp.float32) ** level_of(key_list[1], (NODES, ELEMS), ((1, 32),), -0.2, 0.2)), 0.25, 4.0)
    levels = with_ends(jax.random.randint(key_list[2], (ELEMS,), 0, 4), jax.random.fold_in(key_list[2], 1), 0, 3).astype(jnp.int32)
    local_faces = draw_local_faces(jax.random.fold_in(key_list[10], 71), 0)
    sub_faces = draw_sub_faces(jax.random.fold_in(key_list[10], 71), 0)
    near_faces = draw_near_faces(jax.random.fold_in(key_list[10], 71), 0)
    far_faces = draw_far_faces(jax.random.fold_in(key_list[10], 71), 0)
    child_faces = draw_child_faces(jax.random.fold_in(key_list[10], 71), 0)
    child_peer = draw_child_peer(jax.random.fold_in(key_list[10], 71), 0)
    coarse_faces = draw_coarse_faces(jax.random.fold_in(key_list[10], 71), 0)
    return {"nodal_values": nodal_values, "kappa": kappa, "levels": levels, "local_faces": local_faces, "sub_faces": sub_faces, "near_faces": near_faces, "far_faces": far_faces, "child_faces": child_faces, "child_peer": child_peer, "coarse_faces": coarse_faces}


HIGHEST = lax.Precision.HIGHEST


def legendre_table(points, degree):
    table = [np.ones(points.shape), points.copy()]
    for order in range(2, degree + 1):
        table.append(((2 * order - 1) * points * table[order - 1] - (order - 1) * table[order - 2]) / order)
    return table


def lobatto_points(degree):
    points = np.cos(np.pi * np.arange(degree + 1) / degree)
    for sweep in range(100):
        table = legendre_table(points, degree)
        points = points - (points * table[degree] - table[degree - 1]) / ((degree + 1) * table[degree])
    points = np.sort(points)
    return points, legendre_table(points, degree)[degree]


def node_tables(count):
    degree = count - 1
    points, legendre = lobatto_points(degree)
    weights = 2.0 / (degree * (degree + 1) * legendre ** 2)
    spread = points[:, None] - points[None, :] + np.eye(count)
    derivative = legendre[:, None] / (legendre[None, :] * spread) * (1.0 - np.eye(count))
    derivative[0, 0] = -degree * (degree + 1) / 4.0
    derivative[degree, degree] = degree * (degree + 1) / 4.0
    halves = []
    for side in range(2):
        target = (points + 2.0 * side - 1.0) / 2.0
        matrix = np.ones((count, count))
        for column in range(count):
            for other in range(count):
                if other != column:
                    matrix[:, column] = matrix[:, column] * (target - points[other]) / (points[column] - points[other])
        halves.append(matrix)
    return points, weights, derivative, np.stack(halves)


def stiffness(values, coeffs, level):
    points, weights, derivative, halves = node_tables(NPTS)
    deriv = jnp.asarray(derivative, jnp.float32)
    elems = values.shape[1]
    cube = values.reshape(NPTS, NPTS, NPTS, elems)
    weight_cube = jnp.asarray(weights[:, None, None] * weights[None, :, None] * weights[None, None, :], jnp.float32)
    scale = jnp.power(jnp.float32(0.5), level.astype(jnp.float32))
    geometry = coeffs.reshape(NPTS, NPTS, NPTS, elems) * weight_cube[:, :, :, None] * scale[None, None, None, :]
    first = jnp.einsum("ai,ijkn->ajkn", deriv, cube, precision=HIGHEST)
    first = jnp.einsum("ai,ajkn->ijkn", deriv, geometry * first, precision=HIGHEST)
    second = jnp.einsum("bj,ijkn->ibkn", deriv, cube, precision=HIGHEST)
    second = jnp.einsum("bj,ibkn->ijkn", deriv, geometry * second, precision=HIGHEST)
    third = jnp.einsum("ck,ijkn->ijcn", deriv, cube, precision=HIGHEST)
    third = jnp.einsum("ck,ijcn->ijkn", deriv, geometry * third, precision=HIGHEST)
    return (first + second + third).reshape(NPTS ** 3, elems)


def extract_faces(local):
    elems = local.shape[1]
    cube = local.reshape(NPTS, NPTS, NPTS, elems)
    sides = jnp.stack([cube[0], cube[NPTS - 1], cube[:, 0], cube[:, NPTS - 1], cube[:, :, 0], cube[:, :, NPTS - 1]])
    return sides.reshape(6, NPTS * NPTS, elems).transpose(1, 0, 2).reshape(NPTS * NPTS, 6 * elems)


def add_back(local, total):
    elems = local.shape[1]
    boxes = total.reshape(NPTS * NPTS, 6, elems).transpose(1, 0, 2).reshape(6, NPTS, NPTS, elems)
    cube = local.reshape(NPTS, NPTS, NPTS, elems)
    cube = cube.at[0].add(boxes[0]).at[NPTS - 1].add(boxes[1])
    cube = cube.at[:, 0].add(boxes[2]).at[:, NPTS - 1].add(boxes[3])
    cube = cube.at[:, :, 0].add(boxes[4]).at[:, :, NPTS - 1].add(boxes[5])
    return cube.reshape(NPTS ** 3, elems)


def pick_faces(faces, index_list):
    safe = jnp.maximum(index_list, 0)
    taken = jnp.take(faces, safe, axis=1)
    return taken * (index_list >= 0).astype(faces.dtype)[None, :]


def put_faces(total, index_list, values):
    safe = jnp.where(index_list >= 0, index_list, total.shape[1])
    return total.at[:, safe].add(values, mode="drop")


def restrict(face, part, halves):
    shape = face.shape
    grid = face.reshape(shape[:-2] + (NPTS, NPTS, shape[-1]))
    result = jnp.einsum("ai,bj,...abn->...ijn", halves[part // 2], halves[part % 2], grid, precision=HIGHEST)
    return result.reshape(shape)


def prolong(face, part, halves):
    shape = face.shape
    grid = face.reshape(shape[:-2] + (NPTS, NPTS, shape[-1]))
    result = jnp.einsum("ai,bj,...ijn->...abn", halves[part // 2], halves[part % 2], grid, precision=HIGHEST)
    return result.reshape(shape)


def reference(nodal_values, kappa, levels, local_faces, sub_faces, near_faces, far_faces, child_faces, child_peer, coarse_faces):
    halves = jnp.asarray(node_tables(NPTS)[3], jnp.float32)
    devs = N_DOM * N_SUB
    elems = nodal_values.shape[1] // devs
    square = NPTS * NPTS

    def per_device(array):
        return array.reshape(array.shape[0], devs, elems).transpose(1, 0, 2)

    def tables(array):
        return array.reshape(array.shape[0], devs, array.shape[1] // devs).transpose(1, 0, 2)

    values = per_device(nodal_values)
    coeffs = per_device(kappa)
    level = levels.reshape(devs, elems)
    local = lax.map(lambda items: stiffness(items[0], items[1], items[2]), (values, coeffs, level))
    faces = jax.vmap(extract_faces)(local)
    total = jnp.zeros_like(faces)
    pick_all = jax.vmap(pick_faces)
    put_all = jax.vmap(put_faces)

    pairs = tables(local_faces)
    total = put_all(total, pairs[:, 0], pick_all(faces, pairs[:, 1]))
    total = put_all(total, pairs[:, 1], pick_all(faces, pairs[:, 0]))

    rims = tables(sub_faces)
    width = rims.shape[2]
    down = pick_all(faces, rims[:, 0]).reshape(N_DOM, N_SUB, square, width)
    above = pick_all(faces, rims[:, 1]).reshape(N_DOM, N_SUB, square, width)
    blank = jnp.zeros((N_DOM, 1, square, width), jnp.float32)
    from_lower = jnp.concatenate([blank, above[:, :-1]], axis=1).reshape(devs, square, width)
    from_upper = jnp.concatenate([down[:, 1:], blank], axis=1).reshape(devs, square, width)
    total = put_all(total, rims[:, 0], from_lower)
    total = put_all(total, rims[:, 1], from_upper)

    near = tables(near_faces)
    width = near.shape[2]
    down = pick_all(faces, near[:, 0]).reshape(N_DOM, N_SUB, square, width)
    above = pick_all(faces, near[:, 1]).reshape(N_DOM, N_SUB, square, width)
    blank = jnp.zeros((1, N_SUB, square, width), jnp.float32)
    from_lower = jnp.concatenate([blank, above[:-1]], axis=0).reshape(devs, square, width)
    from_upper = jnp.concatenate([down[1:], blank], axis=0).reshape(devs, square, width)
    total = put_all(total, near[:, 0], from_lower)
    total = put_all(total, near[:, 1], from_upper)

    far = tables(far_faces)
    far_low = pick_all(faces, far[:, 0]).reshape(N_DOM, N_SUB, square, SHIFTS, FAR)
    far_high = pick_all(faces, far[:, 1]).reshape(N_DOM, N_SUB, square, SHIFTS, FAR)
    lower_parts = []
    upper_parts = []
    for step in range(SHIFTS):
        offset = step + 2
        blank = jnp.zeros((offset, N_SUB, square, FAR), jnp.float32)
        lower_parts.append(jnp.concatenate([blank, far_high[:-offset, :, :, step]], axis=0))
        upper_parts.append(jnp.concatenate([far_low[offset:, :, :, step], blank], axis=0))
    from_lower = jnp.stack(lower_parts, axis=3).reshape(devs, square, SHIFTS * FAR)
    from_upper = jnp.stack(upper_parts, axis=3).reshape(devs, square, SHIFTS * FAR)
    total = put_all(total, far[:, 0], from_lower)
    total = put_all(total, far[:, 1], from_upper)

    groups = tables(child_faces)
    count = groups.shape[2]
    peer = child_peer.reshape(N_DOM, N_SUB, count)
    coarse_table = coarse_faces.reshape(devs, N_DOM)
    children = jnp.stack([pick_all(faces, groups[:, part]) for part in range(4)], axis=1)
    projected = sum(restrict(children[:, part], part, halves) for part in range(4))
    projected = projected.reshape(N_DOM, N_SUB, square, count).transpose(0, 1, 3, 2)
    sub_index = lax.iota(jnp.int32, N_SUB)[None, :, None]
    dom_index = lax.iota(jnp.int32, N_DOM)[:, None, None]
    received = jnp.zeros((N_DOM, N_SUB, N_DOM, square), jnp.float32)
    received = received.at[peer, sub_index, dom_index].add(projected)
    received = received.transpose(0, 1, 3, 2).reshape(devs, square, N_DOM)
    coarse = pick_all(faces, coarse_table)
    summed = coarse + received
    total = put_all(total, coarse_table, received)
    spread = summed.reshape(N_DOM, N_SUB, square, N_DOM).transpose(0, 1, 3, 2)
    returned = spread[peer, sub_index, dom_index].transpose(0, 1, 3, 2).reshape(devs, square, count)
    for part in range(4):
        total = put_all(total, groups[:, part], prolong(returned, part, halves) - children[:, part])

    applied = jax.vmap(add_back)(local, total)
    return applied.transpose(1, 0, 2).reshape(NPTS ** 3, devs * elems)
```

```python
import functools

import jax
import jax.numpy as jnp
import numpy as np
from jax import lax
from jax.experimental import pallas as pl
from jax.experimental.pallas import tpu as pltpu
from jax.sharding import PartitionSpec as P

NPTS = 8
FAR = 4
MESH = pl.DeviceIdType.MESH
F32, BF16, I32 = jnp.float32, jnp.bfloat16, jnp.int32


def legendre_table(points, degree):
    table = [np.ones(points.shape), points.copy()]
    for order in range(2, degree + 1):
        table.append(
            ((2 * order - 1) * points * table[order - 1] - (order - 1) * table[order - 2]) / order
        )
    return table


def lobatto_points(degree):
    points = np.cos(np.pi * np.arange(degree + 1) / degree)
    for sweep in range(100):
        table = legendre_table(points, degree)
        points = points - (points * table[degree] - table[degree - 1]) / (
            (degree + 1) * table[degree]
        )
    points = np.sort(points)
    return (points, legendre_table(points, degree)[degree])


def node_tables(count):
    degree = count - 1
    points, legendre = lobatto_points(degree)
    weights = 2.0 / (degree * (degree + 1) * legendre**2)
    spread = points[:, None] - points[None, :] + np.eye(count)
    derivative = legendre[:, None] / (legendre[None, :] * spread) * (1.0 - np.eye(count))
    derivative[0, 0] = -degree * (degree + 1) / 4.0
    derivative[degree, degree] = degree * (degree + 1) / 4.0
    halves = []
    for side in range(2):
        target = (points + 2.0 * side - 1.0) / 2.0
        matrix = np.ones((count, count))
        for column in range(count):
            for other in range(count):
                if other != column:
                    matrix[:, column] = (
                        matrix[:, column]
                        * (target - points[other])
                        / (points[column] - points[other])
                    )
        halves.append(matrix)
    return (points, weights, derivative, np.stack(halves))


POINTS, WEIGHTS, DERIV, HALVES = node_tables(NPTS)


def up(count, unit=8):
    return -(-count // unit) * unit


def halves_of(values):
    high = values.astype(BF16)
    return high, (values - high.astype(F32)).astype(BF16)


def numpy_halves(matrix):
    matrix = np.asarray(matrix, np.float32)
    high = matrix.astype(jnp.bfloat16)
    low = (matrix - high.astype(np.float32)).astype(jnp.bfloat16)
    return high, low


def dot(a, b, dims=((1,), (0,))):
    return lax.dot_general(a, b, (dims, ((), ())), preferred_element_type=F32)


def select(hot, values):
    high, low = halves_of(values)
    return dot(hot, high) + dot(hot, low)


def take_rows(hot, face):
    high, low = halves_of(face)
    dims = ((1,), (1,))
    return dot(hot, high, dims) + dot(hot, low, dims)


def spread_rows(rows, hot):
    high, low = halves_of(rows.T)
    return dot(high, hot) + dot(low, hot)


def product(a, matrix):
    high, low = halves_of(a)
    mhigh, mlow = halves_of(matrix)
    return dot(high, mhigh) + dot(low, mhigh) + dot(high, mlow)


def column(row, padded):
    count = row.shape[1]
    r = lax.broadcasted_iota(I32, (padded, count), 0)
    c = lax.broadcasted_iota(I32, (padded, count), 1)
    spread = jnp.where(r == c, jnp.broadcast_to(row.astype(F32), (padded, count)), 0.0)
    col = jnp.sum(spread, axis=1, keepdims=True)
    inside = lax.broadcasted_iota(I32, (padded, 1), 0) < count
    return jnp.where(inside, col, -1.0)


def hot_rows(columns, base, elems):
    col = columns[0] if len(columns) == 1 else jnp.concatenate(columns, axis=0)
    lane = lax.broadcasted_iota(I32, (col.shape[0], elems), 1).astype(F32)
    return jnp.where(lane == col - float(base), 1.0, 0.0).astype(BF16)


def line(values, matrix):
    half = NPTS // 2
    even = [values[i] + values[NPTS - 1 - i] for i in range(half)]
    odd = [values[i] - values[NPTS - 1 - i] for i in range(half)]
    out = [None] * NPTS
    for a in range(half):
        p = q = None
        for i in range(half):
            s = float((matrix[a, i] + matrix[a, NPTS - 1 - i]) / 2)
            t = float((matrix[a, i] - matrix[a, NPTS - 1 - i]) / 2)
            p = even[i] * s if p is None else p + even[i] * s
            q = odd[i] * t if q is None else q + odd[i] * t
        out[a] = q + p
        out[NPTS - 1 - a] = q - p
    return out


def stencil(matrix):
    big = np.kron(np.eye(16), matrix)
    high, low = numpy_halves(big)
    return np.concatenate([high, high], axis=1), low


def kernel(
    sizes,
    u_hbm,
    kappa_hbm,
    level_hbm,
    local_hbm,
    sub_hbm,
    near_hbm,
    far_hbm,
    child_hbm,
    coarse_hbm,
    deriv_hbm,
    mortar_hbm,
    peer_ref,
    out_hbm,
    level_ref,
    local_ref,
    sub_ref,
    near_ref,
    far_ref,
    child_ref,
    coarse_ref,
    deriv_ref,
    mortar_ref,
    w_ref,
    u_ref,
    k_ref,
    g_ref,
    side_out,
    side_in,
    msg_out,
    msg_in,
    small_sem,
    load_sem,
    side_send,
    side_recv,
    msg_send,
    msg_recv,
):
    n_dom, n_sub = sizes
    parts = u_ref.shape[0]
    elems = parts * 128
    me, sub = lax.axis_index("dom"), lax.axis_index("sub")

    small = [
        pltpu.make_async_copy(source, target, small_sem.at[slot])
        for slot, (source, target) in enumerate(
            [
                (local_hbm, local_ref),
                (sub_hbm, sub_ref),
                (near_hbm, near_ref),
                (far_hbm, far_ref),
                (child_hbm, child_ref),
                (coarse_hbm, coarse_ref),
                (level_hbm, level_ref),
                (deriv_hbm, deriv_ref),
                (mortar_hbm, mortar_ref),
            ]
        )
    ]
    for copy in small[:7]:
        copy.start()

    def load(n, source, target, slot):
        block = source.at[:, pl.ds(n * 128, 128)]
        return pltpu.make_async_copy(block, target.at[n], load_sem.at[slot, n])

    for n in range(parts):
        load(n, u_hbm, u_ref, 0).start()
        load(n, kappa_hbm, k_ref, 1).start()
    for copy in small[7:]:
        copy.start()

    barrier = pltpu.get_barrier_semaphore()

    def greet(step, carry):
        other = lax.rem(me + step, n_dom)
        pl.semaphore_signal(barrier, inc=1, device_id=(other, sub), device_id_type=MESH)
        return carry

    lax.fori_loop(1, n_dom, greet, 0, unroll=n_dom <= 8)

    @pl.when(sub > 0)
    def _():
        pl.semaphore_signal(barrier, inc=1, device_id=(me, sub - 1), device_id_type=MESH)

    @pl.when(sub < n_sub - 1)
    def _():
        pl.semaphore_signal(barrier, inc=1, device_id=(me, sub + 1), device_id_type=MESH)

    def clear(missing, slot):
        @pl.when(missing)
        def _():
            side_in[slot] = jnp.zeros(side_in.shape[1:], F32)

    clear(sub == 0, 0)
    clear(sub == n_sub - 1, 1)
    clear(me == 0, 2)
    clear(me == n_dom - 1, 3)
    msg_in[me] = jnp.zeros(msg_in.shape[1:], F32)

    for copy in small[:7]:
        copy.wait()

    pairs, rim, near = local_ref.shape[1], sub_ref.shape[1], near_ref.shape[1]
    far, groups = far_ref.shape[1], child_ref.shape[1]
    farp, groupp, coarsep = up(far), up(groups), up(n_dom)
    hot0l = hot_rows([column(local_ref[1:2], up(pairs))], 0, elems)
    hot1l = hot_rows([column(local_ref[0:1], up(pairs))], elems, elems)
    hot0s = hot_rows([column(sub_ref[0:1], up(rim))], 0, elems)
    hot1s = hot_rows([column(sub_ref[1:2], up(rim))], elems, elems)
    hot2 = hot_rows([column(near_ref[0:1], up(near))], 2 * elems, elems)
    hot3 = hot_rows([column(near_ref[1:2], up(near))], 3 * elems, elems)
    children = [column(child_ref[m : m + 1], groupp) for m in range(4)]
    hot4 = hot_rows([column(far_ref[0:1], farp)] + children, 4 * elems, elems)
    hot5 = hot_rows(
        [column(far_ref[1:2], farp), column(coarse_ref[...], coarsep)], 5 * elems, elems
    )

    sources = 2 * farp + groupp + coarsep
    rows = 8 * n_dom

    def keys(shape, dim, group_slot, coarse_slot):
        c = lax.broadcasted_iota(I32, shape, dim)
        h = c - farp
        f = jnp.where(c < farp, c, h)
        s, j = lax.shift_right_logical(f, 2), lax.bitwise_and(f, FAR - 1)
        gap = jnp.where(c < farp, -2 - s, s + 2)
        key = jnp.where(f < far, (me + gap) * 8 + j, -1)
        key = jnp.where(c >= 2 * farp, -1, key)
        first = 2 * farp + groupp
        key = jnp.where(c >= first, (c - first) * 8 + coarse_slot, key)
        for slot in range(groups):
            key = jnp.where(c == 2 * farp + slot, peer_ref[slot] * 8 + group_slot, key)
        return key

    def hot(mask):
        return jnp.where(mask, 1.0, 0.0).astype(BF16)

    route = hot(
        lax.broadcasted_iota(I32, (rows, sources), 0) == keys((1, sources), 1, 4, 5)
    )
    unroute = hot(
        lax.broadcasted_iota(I32, (sources, rows), 1) == keys((sources, 1), 0, 5, 4)
    )

    scale = jnp.exp2(-level_ref[...].astype(F32))
    sub8 = lax.broadcasted_iota(I32, (8, elems), 0)
    weight = jnp.zeros((8, elems), F32)
    for k in range(NPTS):
        weight = jnp.where(sub8 == k, float(WEIGHTS[k]), weight)
    weight = weight * scale

    def slab(i, j):
        return pl.ds((i * NPTS + j) * NPTS, NPTS)

    def across(ref, own):
        return jnp.concatenate([ref[n, own, :] for n in range(parts)], axis=1)

    def add_across(own, values):
        for n in range(parts):
            w_ref[n, own, :] += values[:, n * 128 : (n + 1) * 128]

    for n in range(parts):
        load(n, u_hbm, u_ref, 0).wait()
        load(n, kappa_hbm, k_ref, 1).wait()
        here = weight[:, n * 128 : (n + 1) * 128]
        for j in range(NPTS):
            flux = line([u_ref[n, slab(i, j), :] for i in range(NPTS)], DERIV)
            for i in range(NPTS):
                g = k_ref[n, slab(i, j), :] * (here * float(WEIGHTS[i] * WEIGHTS[j]))
                g_ref[n, slab(i, j), :] = g
                flux[i] = flux[i] * g
            flux = line(flux, DERIV.T)
            for i in range(NPTS):
                w_ref[n, slab(i, j), :] = flux[i]
        for i in range(NPTS):
            flux = line([u_ref[n, slab(i, j), :] for j in range(NPTS)], DERIV)
            flux = [flux[j] * g_ref[n, slab(i, j), :] for j in range(NPTS)]
            flux = line(flux, DERIV.T)
            for j in range(NPTS):
                w_ref[n, slab(i, j), :] += flux[j]
    for copy in small[7:]:
        copy.wait()
    block = 128
    for part in range(NPTS**3 // block):
        own = pl.ds(part * block, block)
        high, low = halves_of(across(u_ref, own))
        flux = dot(deriv_ref[0:block, 0 : 2 * block], jnp.concatenate([high, low], axis=0))
        flux += dot(deriv_ref[0:block, 2 * block : 3 * block], high)
        high, low = halves_of(flux * across(g_ref, own))
        turn = dot(deriv_ref[block : 2 * block, 0 : 2 * block], jnp.concatenate([high, low], axis=0))
        turn += dot(deriv_ref[block : 2 * block, 2 * block : 3 * block], high)
        add_across(own, turn)

    square = NPTS * NPTS
    last = NPTS - 1
    low_i, high_i = pl.ds(0, square), pl.ds(last * square, square)
    low_k, high_k = pl.ds(0, square, NPTS), pl.ds(last, square, NPTS)
    face0 = across(w_ref, low_i)
    face1 = across(w_ref, high_i)
    face2 = jnp.concatenate([across(w_ref, slab(i, 0)) for i in range(NPTS)], axis=0)
    face3 = jnp.concatenate([across(w_ref, slab(i, last)) for i in range(NPTS)], axis=0)
    face4 = across(w_ref, low_k)
    face5 = across(w_ref, high_k)

    taken4 = take_rows(hot4, face4)
    taken5 = take_rows(hot5, face5)
    family = [taken4[farp + m * groupp : farp + (m + 1) * groupp] for m in range(4)]
    down = [mortar_ref[m * square : (m + 1) * square, 0:square] for m in range(4)]
    lift = [mortar_ref[m * square : (m + 1) * square, square:] for m in range(4)]
    projected = sum(product(family[m], down[m]) for m in range(4))
    source = jnp.concatenate(
        [taken4[0:farp], taken5[0:farp], projected, taken5[farp:]], axis=0
    )
    message = select(route, source)
    for p in range(n_dom):
        msg_out[p, :, 0:square] = message[8 * p : 8 * p + 8]
    side_out[0, 0:rim, 0:square] = take_rows(hot0s, face0)[0:rim]
    side_out[1, 0:rim, 0:square] = take_rows(hot1s, face1)[0:rim]
    side_out[2, 0:near, 0:square] = take_rows(hot2, face2)[0:near]
    side_out[3, 0:near, 0:square] = take_rows(hot3, face3)[0:near]

    pl.semaphore_wait(
        barrier, n_dom - 1 + (sub > 0).astype(I32) + (sub < n_sub - 1).astype(I32)
    )

    def post(step):
        other = lax.rem(me + step, n_dom)
        return pltpu.make_async_remote_copy(
            src_ref=msg_out.at[other],
            dst_ref=msg_in.at[me],
            send_sem=msg_send.at[other],
            recv_sem=msg_recv.at[me],
            device_id=(other, sub),
            device_id_type=MESH,
        )

    def arrival(step):
        other = lax.rem(me + step, n_dom)
        return pltpu.make_async_remote_copy(
            src_ref=msg_out.at[other],
            dst_ref=msg_in.at[other],
            send_sem=msg_send.at[other],
            recv_sem=msg_recv.at[other],
            device_id=(other, sub),
            device_id_type=MESH,
        )

    sides = [
        (sub > 0, 0, 1, (me, sub - 1)),
        (sub < n_sub - 1, 1, 0, (me, sub + 1)),
        (me > 0, 2, 3, (me - 1, sub)),
        (me < n_dom - 1, 3, 2, (me + 1, sub)),
    ]

    def side_copy(mine, theirs, device):
        return pltpu.make_async_remote_copy(
            src_ref=side_out.at[mine],
            dst_ref=side_in.at[theirs],
            send_sem=side_send.at[mine],
            recv_sem=side_recv.at[theirs],
            device_id=device,
            device_id_type=MESH,
        )

    def start_all(step, carry):
        post(step).start()
        return carry

    lax.fori_loop(1, n_dom, start_all, 0, unroll=n_dom <= 8)
    for there, mine, theirs, device in sides:
        @pl.when(there)
        def _():
            side_copy(mine, theirs, device).start()

    add_across(low_i, spread_rows(take_rows(hot1l, face1), hot0l))
    add_across(high_i, spread_rows(take_rows(hot0l, face0), hot1l))

    for there, mine, theirs, device in sides:
        @pl.when(there)
        def _():
            side_copy(mine, mine, device).wait()

    add_across(low_i, spread_rows(side_in[0, 0:rim, 0:square], hot0s))
    add_across(high_i, spread_rows(side_in[1, 0:rim, 0:square], hot1s))
    add2 = spread_rows(side_in[2, 0:near, 0:square], hot2)
    add3 = spread_rows(side_in[3, 0:near, 0:square], hot3)
    for i in range(NPTS):
        add_across(slab(i, 0), add2[i * NPTS : (i + 1) * NPTS])
        add_across(slab(i, last), add3[i * NPTS : (i + 1) * NPTS])

    def wait_all(step, carry):
        arrival(step).wait()
        return carry

    lax.fori_loop(1, n_dom, wait_all, 0, unroll=n_dom <= 8)
    received = jnp.concatenate([msg_in[p, :, 0:square] for p in range(n_dom)], axis=0)
    back = select(unroute, received)
    summed = back[2 * farp : 2 * farp + groupp] + projected
    add4 = [back[0:farp]] + [product(summed, lift[m]) - family[m] for m in range(4)]
    add5 = [back[farp : 2 * farp], back[2 * farp + groupp :]]
    add_across(low_k, spread_rows(jnp.concatenate(add4, axis=0), hot4))
    add_across(high_k, spread_rows(jnp.concatenate(add5, axis=0), hot5))

    def store(n):
        block = out_hbm.at[:, pl.ds(n * 128, 128)]
        return pltpu.make_async_copy(w_ref.at[n], block, load_sem.at[0, n])

    for n in range(parts):
        store(n).start()
    for n in range(parts):
        store(n).wait()


def body(
    sizes,
    nodal_values,
    kappa,
    levels,
    local_faces,
    sub_faces,
    near_faces,
    far_faces,
    child_faces,
    child_peer,
    coarse_faces,
):
    n_dom, n_sub = sizes
    elems = nodal_values.shape[1]
    double, single = stencil(DERIV)
    double_t, single_t = stencil(DERIV.T)
    deriv = np.concatenate(
        [np.concatenate([double, single], 1), np.concatenate([double_t, single_t], 1)], 0
    )
    krons = [np.kron(HALVES[m // 2], HALVES[m % 2]) for m in range(4)]
    mortar = np.concatenate([np.concatenate([m, m.T], axis=1) for m in krons], axis=0)
    held = (elems // 128, NPTS**3, 128)
    side_rows = up(max(sub_faces.shape[1], near_faces.shape[1]))
    small = [
        levels.reshape(1, elems),
        local_faces,
        sub_faces,
        near_faces,
        far_faces,
        child_faces,
        coarse_faces.reshape(1, n_dom),
        jnp.asarray(deriv, BF16),
        jnp.asarray(mortar, F32),
    ]
    smem = pl.BlockSpec(memory_space=pltpu.SMEM)
    hbm = pl.BlockSpec(memory_space=pl.ANY)
    return pl.pallas_call(
        functools.partial(kernel, sizes),
        out_shape=jax.ShapeDtypeStruct(nodal_values.shape, F32),
        in_specs=[hbm] * 11 + [smem],
        out_specs=hbm,
        scratch_shapes=[pltpu.VMEM(item.shape, item.dtype) for item in small]
        + [
            pltpu.VMEM(held, F32),
            pltpu.VMEM(held, F32),
            pltpu.VMEM(held, F32),
            pltpu.VMEM(held, F32),
            pltpu.VMEM((4, side_rows, 128), F32),
            pltpu.VMEM((4, side_rows, 128), F32),
            pltpu.VMEM((n_dom, 8, 128), F32),
            pltpu.VMEM((n_dom, 8, 128), F32),
            pltpu.SemaphoreType.DMA((len(small),)),
            pltpu.SemaphoreType.DMA((2, held[0])),
            pltpu.SemaphoreType.DMA((4,)),
            pltpu.SemaphoreType.DMA((4,)),
            pltpu.SemaphoreType.DMA((n_dom,)),
            pltpu.SemaphoreType.DMA((n_dom,)),
        ],
        compiler_params=pltpu.CompilerParams(
            collective_id=0, has_side_effects=True, vmem_limit_bytes=60 * 1024 * 1024
        ),
    )(
        nodal_values,
        kappa,
        *small,
        child_peer,
    )


def solution(mesh):
    sizes = (mesh.shape["dom"], mesh.shape["sub"])
    wide = P(None, ("dom", "sub"))
    flat = P(("dom", "sub"))
    in_specs = (wide, wide, flat, wide, wide, wide, wide, wide, flat, flat)
    return jax.shard_map(
        functools.partial(body, sizes),
        mesh=mesh,
        in_specs=in_specs,
        out_specs=wide,
        check_vma=False,
    )
```

```python
import functools

import jax
import jax.numpy as jnp
import numpy as np
from jax import lax
from jax.experimental import pallas as pl
from jax.experimental.pallas import tpu as pltpu
from jax.sharding import PartitionSpec as P

NPTS = 8
FAR = 4
MESH = pl.DeviceIdType.MESH
F32, BF16, I32 = jnp.float32, jnp.bfloat16, jnp.int32


def legendre_table(points, degree):
    table = [np.ones(points.shape), points.copy()]
    for order in range(2, degree + 1):
        table.append(
            ((2 * order - 1) * points * table[order - 1] - (order - 1) * table[order - 2]) / order
        )
    return table


def lobatto_points(degree):
    points = np.cos(np.pi * np.arange(degree + 1) / degree)
    for sweep in range(100):
        table = legendre_table(points, degree)
        points = points - (points * table[degree] - table[degree - 1]) / (
            (degree + 1) * table[degree]
        )
    points = np.sort(points)
    return (points, legendre_table(points, degree)[degree])


def node_tables(count):
    degree = count - 1
    points, legendre = lobatto_points(degree)
    weights = 2.0 / (degree * (degree + 1) * legendre**2)
    spread = points[:, None] - points[None, :] + np.eye(count)
    derivative = legendre[:, None] / (legendre[None, :] * spread) * (1.0 - np.eye(count))
    derivative[0, 0] = -degree * (degree + 1) / 4.0
    derivative[degree, degree] = degree * (degree + 1) / 4.0
    halves = []
    for side in range(2):
        target = (points + 2.0 * side - 1.0) / 2.0
        matrix = np.ones((count, count))
        for column in range(count):
            for other in range(count):
                if other != column:
                    matrix[:, column] = (
                        matrix[:, column]
                        * (target - points[other])
                        / (points[column] - points[other])
                    )
        halves.append(matrix)
    return (points, weights, derivative, np.stack(halves))


POINTS, WEIGHTS, DERIV, HALVES = node_tables(NPTS)


def up(count, unit=8):
    return -(-count // unit) * unit


def halves_of(values):
    high = values.astype(BF16)
    return high, (values - high.astype(F32)).astype(BF16)


def numpy_halves(matrix):
    matrix = np.asarray(matrix, np.float32)
    high = matrix.astype(jnp.bfloat16)
    low = (matrix - high.astype(np.float32)).astype(jnp.bfloat16)
    return high, low


def dot(a, b, dims=((1,), (0,))):
    return lax.dot_general(a, b, (dims, ((), ())), preferred_element_type=F32)


def select(hot, values):
    high, low = halves_of(values)
    return dot(hot, high) + dot(hot, low)


def take_rows(hot, face):
    high, low = halves_of(face)
    dims = ((1,), (1,))
    return dot(hot, high, dims) + dot(hot, low, dims)


def spread_rows(rows, hot):
    high, low = halves_of(rows.T)
    return dot(high, hot) + dot(low, hot)


def product(a, matrix):
    high, low = halves_of(a)
    mhigh, mlow = halves_of(matrix)
    return dot(high, mhigh) + dot(low, mhigh) + dot(high, mlow)


def column(row, padded):
    count = row.shape[1]
    r = lax.broadcasted_iota(I32, (padded, count), 0)
    c = lax.broadcasted_iota(I32, (padded, count), 1)
    spread = jnp.where(r == c, jnp.broadcast_to(row.astype(F32), (padded, count)), 0.0)
    col = jnp.sum(spread, axis=1, keepdims=True)
    inside = lax.broadcasted_iota(I32, (padded, 1), 0) < count
    return jnp.where(inside, col, -1.0)


def hot_rows(columns, base, elems, kind=BF16):
    col = columns[0] if len(columns) == 1 else jnp.concatenate(columns, axis=0)
    lane = lax.broadcasted_iota(I32, (col.shape[0], elems), 1).astype(F32)
    return jnp.where(lane == col - float(base), 1.0, 0.0).astype(kind)


def line(values, matrix):
    half = NPTS // 2
    even = [values[i] + values[NPTS - 1 - i] for i in range(half)]
    odd = [values[i] - values[NPTS - 1 - i] for i in range(half)]
    out = [None] * NPTS
    for a in range(half):
        p = q = None
        for i in range(half):
            s = float((matrix[a, i] + matrix[a, NPTS - 1 - i]) / 2)
            t = float((matrix[a, i] - matrix[a, NPTS - 1 - i]) / 2)
            p = even[i] * s if p is None else p + even[i] * s
            q = odd[i] * t if q is None else q + odd[i] * t
        out[a] = q + p
        out[NPTS - 1 - a] = q - p
    return out


def stencils():
    forth, back = np.kron(np.eye(16), DERIV), np.kron(np.eye(16), DERIV.T)
    ends = np.concatenate([back[0::NPTS], back[NPTS - 1 :: NPTS]], axis=0)
    pieces = [piece for table in (forth, back, ends) for piece in numpy_halves(table)]
    return np.concatenate(pieces, axis=0)


def kernel(
    sizes,
    u_hbm,
    kappa_hbm,
    level_hbm,
    local_hbm,
    sub_hbm,
    near_hbm,
    far_hbm,
    child_hbm,
    coarse_hbm,
    deriv_hbm,
    mortar_hbm,
    peer_ref,
    out_ref,
    level_ref,
    local_ref,
    sub_ref,
    near_ref,
    far_ref,
    child_ref,
    coarse_ref,
    deriv_ref,
    mortar_ref,
    w_ref,
    u_ref,
    k_ref,
    g_ref,
    y_ref,
    side_out,
    side_in,
    msg_out,
    msg_in,
    small_sem,
    load_sem,
    side_send,
    side_recv,
    msg_send,
    msg_recv,
):
    n_dom, n_sub = sizes
    parts = u_ref.shape[0]
    elems = parts * 128
    me, sub = lax.axis_index("dom"), lax.axis_index("sub")

    small = [
        pltpu.make_async_copy(source, target, small_sem.at[slot])
        for slot, (source, target) in enumerate(
            [
                (local_hbm, local_ref),
                (sub_hbm, sub_ref),
                (near_hbm, near_ref),
                (far_hbm, far_ref),
                (child_hbm, child_ref),
                (coarse_hbm, coarse_ref),
                (level_hbm, level_ref),
                (deriv_hbm, deriv_ref),
                (mortar_hbm, mortar_ref),
            ]
        )
    ]
    block = 128
    blocks = NPTS**3 // block

    def load(n, part, source, target, slot):
        own = pl.ds(part * block, block)
        return pltpu.make_async_copy(
            source.at[own, pl.ds(n * 128, 128)], target.at[n, own], load_sem.at[slot, n, part]
        )

    small[7].start()
    for part in range(blocks):
        for n in range(parts):
            load(n, part, u_hbm, u_ref, 0).start()
            load(n, part, kappa_hbm, k_ref, 1).start()
        if part == 0:
            for copy in small[:7]:
                copy.start()
    small[8].start()

    barrier = pltpu.get_barrier_semaphore()

    def greet(step, carry):
        other = lax.rem(me + step, n_dom)
        pl.semaphore_signal(barrier, inc=1, device_id=(other, sub), device_id_type=MESH)
        return carry

    lax.fori_loop(1, n_dom, greet, 0, unroll=n_dom <= 8)

    @pl.when(sub > 0)
    def _():
        pl.semaphore_signal(barrier, inc=1, device_id=(me, sub - 1), device_id_type=MESH)

    @pl.when(sub < n_sub - 1)
    def _():
        pl.semaphore_signal(barrier, inc=1, device_id=(me, sub + 1), device_id_type=MESH)

    def clear(missing, slot):
        @pl.when(missing)
        def _():
            side_in[slot] = jnp.zeros(side_in.shape[1:], F32)

    clear(sub == 0, 0)
    clear(sub == n_sub - 1, 1)
    clear(me == 0, 2)
    clear(me == n_dom - 1, 3)
    msg_in[me] = jnp.zeros(msg_in.shape[1:], F32)

    for copy in small[:7]:
        copy.wait()

    pairs, rim, near = local_ref.shape[1], sub_ref.shape[1], near_ref.shape[1]
    far, groups = far_ref.shape[1], child_ref.shape[1]
    farp, groupp, coarsep = up(far), up(groups), up(n_dom)
    hot0l = hot_rows([column(local_ref[1:2], up(pairs))], 0, elems)
    hot1l = hot_rows([column(local_ref[0:1], up(pairs))], elems, elems)
    hot0s = hot_rows([column(sub_ref[0:1], up(rim))], 0, elems)
    hot1s = hot_rows([column(sub_ref[1:2], up(rim))], elems, elems)
    hot2 = hot_rows([column(near_ref[0:1], up(near))], 2 * elems, elems)
    hot3 = hot_rows([column(near_ref[1:2], up(near))], 3 * elems, elems)
    children = [column(child_ref[m : m + 1], groupp) for m in range(4)]
    hot4f = hot_rows([column(far_ref[0:1], farp)] + children, 4 * elems, elems, F32)
    hot5f = hot_rows(
        [column(far_ref[1:2], farp), column(coarse_ref[...], coarsep)], 5 * elems, elems, F32
    )
    hot4, hot5, hot_kids = hot4f.astype(BF16), hot5f.astype(BF16), hot4f[farp:].astype(BF16)

    sources = 2 * farp + groupp + coarsep
    rows = 8 * n_dom

    def keys(shape, dim, group_slot, coarse_slot):
        c = lax.broadcasted_iota(I32, shape, dim)
        h = c - farp
        f = jnp.where(c < farp, c, h)
        s, j = lax.shift_right_logical(f, 2), lax.bitwise_and(f, FAR - 1)
        gap = jnp.where(c < farp, -2 - s, s + 2)
        key = jnp.where(f < far, (me + gap) * 8 + j, -1)
        key = jnp.where(c >= 2 * farp, -1, key)
        first = 2 * farp + groupp
        key = jnp.where(c >= first, (c - first) * 8 + coarse_slot, key)
        for slot in range(groups):
            key = jnp.where(c == 2 * farp + slot, peer_ref[slot] * 8 + group_slot, key)
        return key

    def hot(mask):
        return jnp.where(mask, 1.0, 0.0).astype(BF16)

    row = lax.broadcasted_iota(I32, (rows, sources), 0)
    route = hot(row == keys((1, sources), 1, 4, 5))
    origin = hot(row == keys((1, sources), 1, 5, 4))

    scale = jnp.exp2(-level_ref[...].astype(F32))
    sub8 = lax.broadcasted_iota(I32, (8, elems), 0)
    weight = jnp.zeros((8, elems), F32)
    for k in range(NPTS):
        weight = jnp.where(sub8 == k, float(WEIGHTS[k]), weight)
    weight = weight * scale

    def slab(i, j):
        return pl.ds((i * NPTS + j) * NPTS, NPTS)

    def across(ref, own):
        return jnp.concatenate([ref[n, own, :] for n in range(parts)], axis=1)

    def add_across(own, values):
        for n in range(parts):
            w_ref[n, own, :] += values[:, n * 128 : (n + 1) * 128]

    small[7].wait()
    turns = [deriv_ref[128 * n : 128 * n + 128, :] for n in range(4)]
    ends = [deriv_ref[512 + 32 * n : 544 + 32 * n, :] for n in range(2)]

    def along(pair, values):
        high, low = halves_of(values)
        both = jnp.concatenate([high, low], axis=0)
        return dot(jnp.concatenate([pair[0], pair[0]], axis=1), both) + dot(pair[1], high)

    low_face, high_face = [], []
    for part in range(blocks):
        own = pl.ds(part * block, block)
        for n in range(parts):
            load(n, part, u_hbm, u_ref, 0).wait()
            load(n, part, kappa_hbm, k_ref, 1).wait()
        for n in range(parts):
            here = weight[:, n * 128 : (n + 1) * 128]
            for i in range(part * 2, part * 2 + 2):
                for j in range(NPTS):
                    g_ref[n, slab(i, j), :] = k_ref[n, slab(i, j), :] * (
                        here * float(WEIGHTS[i] * WEIGHTS[j])
                    )
        flux = along(turns[0:2], across(u_ref, own)) * across(g_ref, own)
        for n in range(parts):
            y_ref[n, own, :] = flux[:, n * 128 : (n + 1) * 128]
        end = along(ends, flux)
        low_face.append(end[0:16])
        high_face.append(end[16:32])

    square = NPTS * NPTS
    last = NPTS - 1
    low_i, high_i = pl.ds(0, square), pl.ds(last * square, square)
    low_k, high_k = pl.ds(0, square, NPTS), pl.ds(last, square, NPTS)
    u4, u5, g4, g5 = (across(r, k) for r in (u_ref, g_ref) for k in (low_k, high_k))
    flux = along(turns[0:2], jnp.concatenate([u4, u5], axis=0))
    flux = along(turns[2:4], flux * jnp.concatenate([g4, g5], axis=0))

    def across_i(u, g):
        part = line([u[i * NPTS : (i + 1) * NPTS] for i in range(NPTS)], DERIV)
        part = [part[i] * g[i * NPTS : (i + 1) * NPTS] for i in range(NPTS)]
        return jnp.concatenate(line(part, DERIV.T), axis=0)

    face4 = jnp.concatenate(low_face, axis=0) + flux[0:square] + across_i(u4, g4)
    face5 = jnp.concatenate(high_face, axis=0) + flux[square:] + across_i(u5, g5)

    small[8].wait()
    taken4 = take_rows(hot4, face4)
    taken5 = take_rows(hot5, face5)
    family = [taken4[farp + m * groupp : farp + (m + 1) * groupp] for m in range(4)]
    down = [mortar_ref[m * square : (m + 1) * square, 0:square] for m in range(4)]
    lift = [mortar_ref[m * square : (m + 1) * square, square:] for m in range(4)]
    projected = sum(product(family[m], down[m]) for m in range(4))
    source = jnp.concatenate(
        [taken4[0:farp], taken5[0:farp], projected, taken5[farp:]], axis=0
    )
    message = select(route, source)
    for p in range(n_dom):
        msg_out[p, :, 0:square] = message[8 * p : 8 * p + 8]
    pl.semaphore_wait(
        barrier, n_dom - 1 + (sub > 0).astype(I32) + (sub < n_sub - 1).astype(I32)
    )

    def post(step):
        other = lax.rem(me + step, n_dom)
        return pltpu.make_async_remote_copy(
            src_ref=msg_out.at[other],
            dst_ref=msg_in.at[me],
            send_sem=msg_send.at[other],
            recv_sem=msg_recv.at[me],
            device_id=(other, sub),
            device_id_type=MESH,
        )

    def arrival(step):
        other = lax.rem(me + step, n_dom)
        return pltpu.make_async_remote_copy(
            src_ref=msg_out.at[other],
            dst_ref=msg_in.at[other],
            send_sem=msg_send.at[other],
            recv_sem=msg_recv.at[other],
            device_id=(other, sub),
            device_id_type=MESH,
        )

    sides = [
        (sub > 0, 0, 1, (me, sub - 1)),
        (sub < n_sub - 1, 1, 0, (me, sub + 1)),
        (me > 0, 2, 3, (me - 1, sub)),
        (me < n_dom - 1, 3, 2, (me + 1, sub)),
    ]

    def side_copy(mine, theirs, device):
        return pltpu.make_async_remote_copy(
            src_ref=side_out.at[mine],
            dst_ref=side_in.at[theirs],
            send_sem=side_send.at[mine],
            recv_sem=side_recv.at[theirs],
            device_id=device,
            device_id_type=MESH,
        )

    def start_all(step, carry):
        post(step).start()
        return carry

    lax.fori_loop(1, n_dom, start_all, 0, unroll=n_dom <= 8)

    for part in range(blocks):
        own = pl.ds(part * block, block)
        turn = along(turns[2:4], across(y_ref, own))
        for n in range(parts):
            w_ref[n, own, :] = turn[:, n * 128 : (n + 1) * 128]
    for n in range(parts):
        for j in range(NPTS):
            flux = line([u_ref[n, slab(i, j), :] for i in range(NPTS)], DERIV)
            flux = [flux[i] * g_ref[n, slab(i, j), :] for i in range(NPTS)]
            flux = line(flux, DERIV.T)
            for i in range(NPTS):
                w_ref[n, slab(i, j), :] += flux[i]
        for i in range(NPTS):
            flux = line([u_ref[n, slab(i, j), :] for j in range(NPTS)], DERIV)
            flux = [flux[j] * g_ref[n, slab(i, j), :] for j in range(NPTS)]
            flux = line(flux, DERIV.T)
            for j in range(NPTS):
                w_ref[n, slab(i, j), :] += flux[j]
    face0 = across(w_ref, low_i)
    face1 = across(w_ref, high_i)
    face2 = jnp.concatenate([across(w_ref, slab(i, 0)) for i in range(NPTS)], axis=0)
    face3 = jnp.concatenate([across(w_ref, slab(i, last)) for i in range(NPTS)], axis=0)
    side_out[0, 0:rim, 0:square] = take_rows(hot0s, face0)[0:rim]
    side_out[1, 0:rim, 0:square] = take_rows(hot1s, face1)[0:rim]
    side_out[2, 0:near, 0:square] = take_rows(hot2, face2)[0:near]
    side_out[3, 0:near, 0:square] = take_rows(hot3, face3)[0:near]

    for there, mine, theirs, device in sides:
        @pl.when(there)
        def _():
            side_copy(mine, theirs, device).start()

    share = [product(projected, lift[m]) - family[m] for m in range(4)]
    add_across(low_k, spread_rows(jnp.concatenate(share, axis=0), hot_kids))

    def rows_at(first, values):
        pieces = []
        if first:
            pieces.append(jnp.zeros((first, elems), F32))
        pieces.append(values)
        if first + values.shape[0] < sources:
            pieces.append(jnp.zeros((sources - first - values.shape[0], elems), F32))
        return pieces[0] if len(pieces) == 1 else jnp.concatenate(pieces, axis=0)

    def land(values):
        return dot(origin, values.astype(BF16)).astype(BF16)

    land4 = land(rows_at(0, hot4f[0:farp]))
    land5 = land(rows_at(farp, hot5f[0:farp]) + rows_at(2 * farp + groupp, hot5f[farp:]))
    first = farp
    land_kids = []
    for m in range(4):
        land_kids.append(land(rows_at(2 * farp, hot4f[first : first + groupp])))
        first += groupp
    kron = halves_of(mortar_ref[:, 0:square])

    add_across(low_i, spread_rows(take_rows(hot1l, face1), hot0l))
    add_across(high_i, spread_rows(take_rows(hot0l, face0), hot1l))

    for there, mine, theirs, device in sides:
        @pl.when(there)
        def _():
            side_copy(mine, mine, device).wait()

    add_across(low_i, spread_rows(side_in[0, 0:rim, 0:square], hot0s))
    add_across(high_i, spread_rows(side_in[1, 0:rim, 0:square], hot1s))
    add2 = spread_rows(side_in[2, 0:near, 0:square], hot2)
    add3 = spread_rows(side_in[3, 0:near, 0:square], hot3)
    for i in range(NPTS):
        add_across(slab(i, 0), add2[i * NPTS : (i + 1) * NPTS])
        add_across(slab(i, last), add3[i * NPTS : (i + 1) * NPTS])

    def wait_all(step, carry):
        arrival(step).wait()
        return carry

    lax.fori_loop(1, n_dom, wait_all, 0, unroll=n_dom <= 8)
    received = jnp.concatenate([msg_in[p, :, 0:square] for p in range(n_dom)], axis=0)
    high, low = halves_of(received.T)
    add5 = dot(high, land5) + dot(low, land5)
    add4 = dot(high, land4) + dot(low, land4)
    lifted = dot(kron[0], high) + dot(kron[0], low) + dot(kron[1], high)
    for m in range(4):
        high, low = halves_of(lifted[m * square : (m + 1) * square])
        add4 += dot(high, land_kids[m]) + dot(low, land_kids[m])
    add_across(high_k, add5)
    add_across(low_k, add4)
    for n in range(parts):
        out_ref[:, n * 128 : (n + 1) * 128] = w_ref[n]


def body(
    sizes,
    nodal_values,
    kappa,
    levels,
    local_faces,
    sub_faces,
    near_faces,
    far_faces,
    child_faces,
    child_peer,
    coarse_faces,
):
    n_dom, n_sub = sizes
    elems = nodal_values.shape[1]
    krons = [np.kron(HALVES[m // 2], HALVES[m % 2]) for m in range(4)]
    mortar = np.concatenate([np.concatenate([m, m.T], axis=1) for m in krons], axis=0)
    held = (elems // 128, NPTS**3, 128)
    side_rows = up(max(sub_faces.shape[1], near_faces.shape[1]))
    small = [
        levels.reshape(1, elems),
        local_faces,
        sub_faces,
        near_faces,
        far_faces,
        child_faces,
        coarse_faces.reshape(1, n_dom),
        jnp.asarray(stencils(), BF16),
        jnp.asarray(mortar, F32),
    ]
    smem = pl.BlockSpec(memory_space=pltpu.SMEM)
    hbm = pl.BlockSpec(memory_space=pltpu.HBM)
    vmem = pl.BlockSpec(memory_space=pltpu.VMEM)
    return pl.pallas_call(
        functools.partial(kernel, sizes),
        out_shape=pltpu.VMEM(nodal_values.shape, F32),
        in_specs=[hbm] * 11 + [smem],
        out_specs=vmem,
        scratch_shapes=[pltpu.VMEM(item.shape, item.dtype) for item in small]
        + [
            pltpu.VMEM(held, F32),
            pltpu.VMEM(held, F32),
            pltpu.VMEM(held, F32),
            pltpu.VMEM(held, F32),
            pltpu.VMEM(held, F32),
            pltpu.VMEM((4, side_rows, 128), F32),
            pltpu.VMEM((4, side_rows, 128), F32),
            pltpu.VMEM((n_dom, 8, 128), F32),
            pltpu.VMEM((n_dom, 8, 128), F32),
            pltpu.SemaphoreType.DMA((len(small),)),
            pltpu.SemaphoreType.DMA((2, held[0], NPTS**3 // 128)),
            pltpu.SemaphoreType.DMA((4,)),
            pltpu.SemaphoreType.DMA((4,)),
            pltpu.SemaphoreType.DMA((n_dom,)),
            pltpu.SemaphoreType.DMA((n_dom,)),
        ],
        compiler_params=pltpu.CompilerParams(
            collective_id=0, has_side_effects=True, vmem_limit_bytes=60 * 1024 * 1024
        ),
    )(
        nodal_values,
        kappa,
        *small,
        child_peer,
    )


def solution(mesh):
    sizes = (mesh.shape["dom"], mesh.shape["sub"])
    wide = P(None, ("dom", "sub"))
    flat = P(("dom", "sub"))
    in_specs = (wide, wide, flat, wide, wide, wide, wide, wide, flat, flat)
    return jax.shard_map(
        functools.partial(body, sizes),
        mesh=mesh,
        in_specs=in_specs,
        out_specs=wide,
        check_vma=False,
    )
```

```python
import functools

import jax
import jax.numpy as jnp
import numpy as np
from jax import lax
from jax.experimental import pallas as pl
from jax.experimental.pallas import tpu as pltpu
from jax.sharding import PartitionSpec as P

NPTS = 8
FAR = 4
MESH = pl.DeviceIdType.MESH
F32, BF16, I32 = jnp.float32, jnp.bfloat16, jnp.int32


def legendre_table(points, degree):
    table = [np.ones(points.shape), points.copy()]
    for order in range(2, degree + 1):
        table.append(
            ((2 * order - 1) * points * table[order - 1] - (order - 1) * table[order - 2]) / order
        )
    return table


def lobatto_points(degree):
    points = np.cos(np.pi * np.arange(degree + 1) / degree)
    for sweep in range(100):
        table = legendre_table(points, degree)
        points = points - (points * table[degree] - table[degree - 1]) / (
            (degree + 1) * table[degree]
        )
    points = np.sort(points)
    return (points, legendre_table(points, degree)[degree])


def node_tables(count):
    degree = count - 1
    points, legendre = lobatto_points(degree)
    weights = 2.0 / (degree * (degree + 1) * legendre**2)
    spread = points[:, None] - points[None, :] + np.eye(count)
    derivative = legendre[:, None] / (legendre[None, :] * spread) * (1.0 - np.eye(count))
    derivative[0, 0] = -degree * (degree + 1) / 4.0
    derivative[degree, degree] = degree * (degree + 1) / 4.0
    halves = []
    for side in range(2):
        target = (points + 2.0 * side - 1.0) / 2.0
        matrix = np.ones((count, count))
        for column in range(count):
            for other in range(count):
                if other != column:
                    matrix[:, column] = (
                        matrix[:, column]
                        * (target - points[other])
                        / (points[column] - points[other])
                    )
        halves.append(matrix)
    return (points, weights, derivative, np.stack(halves))


POINTS, WEIGHTS, DERIV, HALVES = node_tables(NPTS)


def up(count, unit=8):
    return -(-count // unit) * unit


def halves_of(values):
    high = values.astype(BF16)
    return high, (values - high.astype(F32)).astype(BF16)


def numpy_halves(matrix):
    matrix = np.asarray(matrix, np.float32)
    high = matrix.astype(jnp.bfloat16)
    low = (matrix - high.astype(np.float32)).astype(jnp.bfloat16)
    return high, low


def dot(a, b, dims=((1,), (0,))):
    return lax.dot_general(a, b, (dims, ((), ())), preferred_element_type=F32)


def select(hot, values):
    high, low = halves_of(values)
    return dot(hot, high) + dot(hot, low)


def take_rows(hot, face):
    high, low = halves_of(face)
    dims = ((1,), (1,))
    return dot(hot, high, dims) + dot(hot, low, dims)


def spread_rows(rows, hot):
    high, low = halves_of(rows.T)
    return dot(high, hot) + dot(low, hot)


def product(a, matrix):
    high, low = halves_of(a)
    mhigh, mlow = halves_of(matrix)
    return dot(high, mhigh) + dot(low, mhigh) + dot(high, mlow)


def column(row, padded):
    count = row.shape[1]
    r = lax.broadcasted_iota(I32, (padded, count), 0)
    c = lax.broadcasted_iota(I32, (padded, count), 1)
    spread = jnp.where(r == c, jnp.broadcast_to(row.astype(F32), (padded, count)), 0.0)
    col = jnp.sum(spread, axis=1, keepdims=True)
    inside = lax.broadcasted_iota(I32, (padded, 1), 0) < count
    return jnp.where(inside, col, -1.0)


def hot_rows(columns, base, elems, kind=BF16):
    col = columns[0] if len(columns) == 1 else jnp.concatenate(columns, axis=0)
    lane = lax.broadcasted_iota(I32, (col.shape[0], elems), 1).astype(F32)
    return jnp.where(lane == col - float(base), 1.0, 0.0).astype(kind)


def line(values, matrix):
    half = NPTS // 2
    even = [values[i] + values[NPTS - 1 - i] for i in range(half)]
    odd = [values[i] - values[NPTS - 1 - i] for i in range(half)]
    out = [None] * NPTS
    for a in range(half):
        p = q = None
        for i in range(half):
            s = float((matrix[a, i] + matrix[a, NPTS - 1 - i]) / 2)
            t = float((matrix[a, i] - matrix[a, NPTS - 1 - i]) / 2)
            p = even[i] * s if p is None else p + even[i] * s
            q = odd[i] * t if q is None else q + odd[i] * t
        out[a] = q + p
        out[NPTS - 1 - a] = q - p
    return out


def stencils():
    forth, back = np.kron(np.eye(16), DERIV), np.kron(np.eye(16), DERIV.T)
    ends = np.concatenate([back[0::NPTS], back[NPTS - 1 :: NPTS]], axis=0)
    pieces = [piece for table in (forth, back, ends) for piece in numpy_halves(table)]
    return np.concatenate(pieces, axis=0)


def kernel(
    sizes,
    u_hbm,
    kappa_hbm,
    level_hbm,
    local_hbm,
    sub_hbm,
    near_hbm,
    far_hbm,
    child_hbm,
    coarse_hbm,
    deriv_hbm,
    mortar_hbm,
    peer_hbm,
    out_ref,
    level_ref,
    local_ref,
    sub_ref,
    near_ref,
    far_ref,
    child_ref,
    coarse_ref,
    deriv_ref,
    mortar_ref,
    peer_ref,
    w_ref,
    u_ref,
    k_ref,
    g_ref,
    y_ref,
    side_out,
    side_in,
    msg_out,
    msg_in,
    small_sem,
    load_sem,
    side_send,
    side_recv,
    msg_send,
    msg_recv,
):
    n_dom, n_sub = sizes
    parts = u_ref.shape[0]
    elems = parts * 128
    me, sub = lax.axis_index("dom"), lax.axis_index("sub")

    small = [
        pltpu.make_async_copy(source, target, small_sem.at[slot])
        for slot, (source, target) in enumerate(
            [
                (local_hbm, local_ref),
                (sub_hbm, sub_ref),
                (near_hbm, near_ref),
                (far_hbm, far_ref),
                (child_hbm, child_ref),
                (coarse_hbm, coarse_ref),
                (level_hbm, level_ref),
                (deriv_hbm, deriv_ref),
                (mortar_hbm, mortar_ref),
                (peer_hbm, peer_ref),
            ]
        )
    ]
    block = 128
    blocks = NPTS**3 // block

    def load(n, part, source, target, slot):
        own = pl.ds(part * block, block)
        return pltpu.make_async_copy(
            source.at[own, pl.ds(n * 128, 128)], target.at[n, own], load_sem.at[slot, n, part]
        )

    for copy in small[:7] + small[9:]:
        copy.start()
    small[7].start()
    for part in range(blocks):
        for n in range(parts):
            load(n, part, u_hbm, u_ref, 0).start()
            load(n, part, kappa_hbm, k_ref, 1).start()
    small[8].start()

    barrier = pltpu.get_barrier_semaphore()

    def greet(step, carry):
        other = lax.rem(me + step, n_dom)
        pl.semaphore_signal(barrier, inc=1, device_id=(other, sub), device_id_type=MESH)
        return carry

    lax.fori_loop(1, n_dom, greet, 0, unroll=n_dom <= 8)

    @pl.when(sub > 0)
    def _():
        pl.semaphore_signal(barrier, inc=1, device_id=(me, sub - 1), device_id_type=MESH)

    @pl.when(sub < n_sub - 1)
    def _():
        pl.semaphore_signal(barrier, inc=1, device_id=(me, sub + 1), device_id_type=MESH)

    def clear(missing, slot):
        @pl.when(missing)
        def _():
            side_in[slot] = jnp.zeros(side_in.shape[1:], F32)

    clear(sub == 0, 0)
    clear(sub == n_sub - 1, 1)
    clear(me == 0, 2)
    clear(me == n_dom - 1, 3)
    msg_in[me] = jnp.zeros(msg_in.shape[1:], F32)

    for copy in small[:7] + small[9:]:
        copy.wait()

    pairs, rim, near = local_ref.shape[1], sub_ref.shape[1], near_ref.shape[1]
    far, groups = far_ref.shape[1], child_ref.shape[1]
    farp, groupp, coarsep = up(far), up(groups), up(n_dom)
    hot0l = hot_rows([column(local_ref[1:2], up(pairs))], 0, elems)
    hot1l = hot_rows([column(local_ref[0:1], up(pairs))], elems, elems)
    hot0s = hot_rows([column(sub_ref[0:1], up(rim))], 0, elems)
    hot1s = hot_rows([column(sub_ref[1:2], up(rim))], elems, elems)
    hot2 = hot_rows([column(near_ref[0:1], up(near))], 2 * elems, elems)
    hot3 = hot_rows([column(near_ref[1:2], up(near))], 3 * elems, elems)
    children = [column(child_ref[m : m + 1], groupp) for m in range(4)]
    hot4f = hot_rows([column(far_ref[0:1], farp)] + children, 4 * elems, elems, F32)
    hot5f = hot_rows(
        [column(far_ref[1:2], farp), column(coarse_ref[...], coarsep)], 5 * elems, elems, F32
    )
    hot4, hot5, hot_kids = hot4f.astype(BF16), hot5f.astype(BF16), hot4f[farp:].astype(BF16)

    sources = 2 * farp + groupp + coarsep
    rows = 8 * n_dom

    def keys(shape, dim, group_slot, coarse_slot):
        c = lax.broadcasted_iota(I32, shape, dim)
        h = c - farp
        f = jnp.where(c < farp, c, h)
        s, j = lax.shift_right_logical(f, 2), lax.bitwise_and(f, FAR - 1)
        gap = jnp.where(c < farp, -2 - s, s + 2)
        key = jnp.where(f < far, (me + gap) * 8 + j, -1)
        key = jnp.where(c >= 2 * farp, -1, key)
        first = 2 * farp + groupp
        key = jnp.where(c >= first, (c - first) * 8 + coarse_slot, key)
        for slot in range(groups):
            key = jnp.where(c == 2 * farp + slot, peer_ref[slot] * 8 + group_slot, key)
        return key

    def hot(mask):
        return jnp.where(mask, 1.0, 0.0).astype(BF16)

    row = lax.broadcasted_iota(I32, (rows, sources), 0)
    route = hot(row == keys((1, sources), 1, 4, 5))
    origin = hot(row == keys((1, sources), 1, 5, 4))

    def rows_at(first, values):
        pieces = []
        if first:
            pieces.append(jnp.zeros((first, elems), F32))
        pieces.append(values)
        if first + values.shape[0] < sources:
            pieces.append(jnp.zeros((sources - first - values.shape[0], elems), F32))
        return pieces[0] if len(pieces) == 1 else jnp.concatenate(pieces, axis=0)

    def land(where, values):
        return dot(where, values.astype(BF16)).astype(BF16)

    at_five = rows_at(farp, hot5f[0:farp]) + rows_at(2 * farp + groupp, hot5f[farp:])
    send5 = land(route, at_five)
    send4 = [dot(route, rows_at(0, hot4f[0:farp]).astype(BF16))]
    dom_row = lax.broadcasted_iota(I32, (n_dom, groupp), 0)
    dom_slot = lax.broadcasted_iota(I32, (n_dom, groupp), 1)
    named = jnp.full((n_dom, groupp), -1, I32)
    for slot in range(groups):
        named = jnp.where(dom_slot == slot, peer_ref[slot], named)
    named = hot(named == dom_row)
    for m in range(4):
        first = farp + m * groupp
        send4.append(dot(named, hot4f[first : first + groupp].astype(BF16)))
    send4 = jnp.concatenate(send4, axis=0).astype(BF16)

    scale = jnp.exp2(-level_ref[...].astype(F32))
    sub8 = lax.broadcasted_iota(I32, (8, elems), 0)
    weight = jnp.zeros((8, elems), F32)
    for k in range(NPTS):
        weight = jnp.where(sub8 == k, float(WEIGHTS[k]), weight)
    weight = weight * scale

    def slab(i, j):
        return pl.ds((i * NPTS + j) * NPTS, NPTS)

    def across(ref, own):
        return jnp.concatenate([ref[n, own, :] for n in range(parts)], axis=1)

    def add_across(own, values):
        for n in range(parts):
            w_ref[n, own, :] += values[:, n * 128 : (n + 1) * 128]

    small[7].wait()
    turns = [deriv_ref[128 * n : 128 * n + 128, :] for n in range(4)]
    ends = [deriv_ref[512 + 32 * n : 544 + 32 * n, :] for n in range(2)]

    def along(pair, values):
        high, low = halves_of(values)
        both = jnp.concatenate([high, low], axis=0)
        return dot(jnp.concatenate([pair[0], pair[0]], axis=1), both) + dot(pair[1], high)

    low_face, high_face = [], []
    for part in range(blocks):
        own = pl.ds(part * block, block)
        if part == 0:
            for n in range(blocks * parts):
                load(n // blocks, n % blocks, u_hbm, u_ref, 0).wait()
                load(n // blocks, n % blocks, kappa_hbm, k_ref, 1).wait()
        if part == 0:
            small[8].wait()
        for n in range(parts):
            here = weight[:, n * 128 : (n + 1) * 128]
            for i in range(part * 2, part * 2 + 2):
                for j in range(NPTS):
                    g_ref[n, slab(i, j), :] = k_ref[n, slab(i, j), :] * (
                        here * float(WEIGHTS[i] * WEIGHTS[j])
                    )
        flux = along(turns[0:2], across(u_ref, own)) * across(g_ref, own)
        for n in range(parts):
            y_ref[n, own, :] = flux[:, n * 128 : (n + 1) * 128]
        end = along(ends, flux)
        low_face.append(end[0:16])
        high_face.append(end[16:32])

    square = NPTS * NPTS
    last = NPTS - 1
    low_i, high_i = pl.ds(0, square), pl.ds(last * square, square)
    low_k, high_k = pl.ds(0, square, NPTS), pl.ds(last, square, NPTS)
    u4, u5, g4, g5 = (across(r, k) for r in (u_ref, g_ref) for k in (low_k, high_k))
    flux = along(turns[0:2], jnp.concatenate([u4, u5], axis=0))
    flux = along(turns[2:4], flux * jnp.concatenate([g4, g5], axis=0))

    def across_i(u, g):
        part = line([u[i * NPTS : (i + 1) * NPTS] for i in range(NPTS)], DERIV)
        part = [part[i] * g[i * NPTS : (i + 1) * NPTS] for i in range(NPTS)]
        return jnp.concatenate(line(part, DERIV.T), axis=0)

    face4 = jnp.concatenate(low_face, axis=0) + flux[0:square] + across_i(u4, g4)
    face5 = jnp.concatenate(high_face, axis=0) + flux[square:] + across_i(u5, g5)

    down = [mortar_ref[m * square : (m + 1) * square, 0:square] for m in range(4)]
    lift = [mortar_ref[m * square : (m + 1) * square, square:] for m in range(4)]
    message = take_rows(send5, face5)
    taken4 = take_rows(send4, face4)
    message += taken4[0:rows]
    kids = [taken4[rows + m * n_dom : rows + (m + 1) * n_dom] for m in range(4)]
    sent = sum(product(kids[m], down[m]) for m in range(4))
    for p in range(n_dom):
        msg_out[p, :, 0:square] = message[8 * p : 8 * p + 8]
        msg_out[p, 4:5, 0:square] = sent[p : p + 1]

    pl.semaphore_wait(
        barrier, n_dom - 1 + (sub > 0).astype(I32) + (sub < n_sub - 1).astype(I32)
    )

    def post(step):
        other = lax.rem(me + step, n_dom)
        return pltpu.make_async_remote_copy(
            src_ref=msg_out.at[other],
            dst_ref=msg_in.at[me],
            send_sem=msg_send.at[other],
            recv_sem=msg_recv.at[me],
            device_id=(other, sub),
            device_id_type=MESH,
        )

    def arrival(step):
        other = lax.rem(me + step, n_dom)
        return pltpu.make_async_remote_copy(
            src_ref=msg_out.at[other],
            dst_ref=msg_in.at[other],
            send_sem=msg_send.at[other],
            recv_sem=msg_recv.at[other],
            device_id=(other, sub),
            device_id_type=MESH,
        )

    sides = [
        (sub > 0, 0, 1, (me, sub - 1)),
        (sub < n_sub - 1, 1, 0, (me, sub + 1)),
        (me > 0, 2, 3, (me - 1, sub)),
        (me < n_dom - 1, 3, 2, (me + 1, sub)),
    ]

    def side_copy(mine, theirs, device):
        return pltpu.make_async_remote_copy(
            src_ref=side_out.at[mine],
            dst_ref=side_in.at[theirs],
            send_sem=side_send.at[mine],
            recv_sem=side_recv.at[theirs],
            device_id=device,
            device_id_type=MESH,
        )

    def start_all(step, carry):
        post(step).start()
        return carry

    lax.fori_loop(1, n_dom, start_all, 0, unroll=n_dom <= 8)

    for part in range(blocks):
        own = pl.ds(part * block, block)
        turn = along(turns[2:4], across(y_ref, own))
        for n in range(parts):
            w_ref[n, own, :] = turn[:, n * 128 : (n + 1) * 128]
    for n in range(parts):
        for j in range(NPTS):
            flux = line([u_ref[n, slab(i, j), :] for i in range(NPTS)], DERIV)
            flux = [flux[i] * g_ref[n, slab(i, j), :] for i in range(NPTS)]
            flux = line(flux, DERIV.T)
            for i in range(NPTS):
                w_ref[n, slab(i, j), :] += flux[i]
        for i in range(NPTS):
            flux = line([u_ref[n, slab(i, j), :] for j in range(NPTS)], DERIV)
            flux = [flux[j] * g_ref[n, slab(i, j), :] for j in range(NPTS)]
            flux = line(flux, DERIV.T)
            for j in range(NPTS):
                w_ref[n, slab(i, j), :] += flux[j]
    face0 = across(w_ref, low_i)
    face1 = across(w_ref, high_i)
    face2 = jnp.concatenate([across(w_ref, slab(i, 0)) for i in range(NPTS)], axis=0)
    face3 = jnp.concatenate([across(w_ref, slab(i, last)) for i in range(NPTS)], axis=0)
    side_out[0, 0:rim, 0:square] = take_rows(hot0s, face0)[0:rim]
    side_out[1, 0:rim, 0:square] = take_rows(hot1s, face1)[0:rim]
    side_out[2, 0:near, 0:square] = take_rows(hot2, face2)[0:near]
    side_out[3, 0:near, 0:square] = take_rows(hot3, face3)[0:near]

    for there, mine, theirs, device in sides:
        @pl.when(there)
        def _():
            side_copy(mine, theirs, device).start()

    taken4 = take_rows(hot_kids, face4)
    family = [taken4[m * groupp : (m + 1) * groupp] for m in range(4)]
    projected = sum(product(family[m], down[m]) for m in range(4))

    land4 = land(origin, rows_at(0, hot4f[0:farp]))
    land5 = land(origin, at_five)
    first = farp
    land_kids = []
    for m in range(4):
        land_kids.append(land(origin, rows_at(2 * farp, hot4f[first : first + groupp])))
        first += groupp

    share = [product(projected, lift[m]) - family[m] for m in range(4)]
    add_across(low_k, spread_rows(jnp.concatenate(share, axis=0), hot_kids))

    kron = halves_of(mortar_ref[:, 0:square])

    add_across(low_i, spread_rows(take_rows(hot1l, face1), hot0l))
    add_across(high_i, spread_rows(take_rows(hot0l, face0), hot1l))

    for there, mine, theirs, device in sides:
        @pl.when(there)
        def _():
            side_copy(mine, mine, device).wait()

    add_across(low_i, spread_rows(side_in[0, 0:rim, 0:square], hot0s))
    add_across(high_i, spread_rows(side_in[1, 0:rim, 0:square], hot1s))
    add2 = spread_rows(side_in[2, 0:near, 0:square], hot2)
    add3 = spread_rows(side_in[3, 0:near, 0:square], hot3)
    for i in range(NPTS):
        add_across(slab(i, 0), add2[i * NPTS : (i + 1) * NPTS])
        add_across(slab(i, last), add3[i * NPTS : (i + 1) * NPTS])

    def wait_all(step, carry):
        arrival(step).wait()
        return carry

    lax.fori_loop(1, n_dom, wait_all, 0, unroll=n_dom <= 8)
    received = jnp.concatenate([msg_in[p, :, 0:square] for p in range(n_dom)], axis=0)
    high, low = halves_of(received.T)
    add5 = dot(high, land5) + dot(low, land5)
    add4 = dot(high, land4) + dot(low, land4)
    lifted = dot(kron[0], high) + dot(kron[0], low) + dot(kron[1], high)
    for m in range(4):
        high, low = halves_of(lifted[m * square : (m + 1) * square])
        add4 += dot(high, land_kids[m]) + dot(low, land_kids[m])
    add_across(high_k, add5)
    add_across(low_k, add4)
    for n in range(parts):
        out_ref[:, n * 128 : (n + 1) * 128] = w_ref[n]


def body(
    sizes,
    nodal_values,
    kappa,
    levels,
    local_faces,
    sub_faces,
    near_faces,
    far_faces,
    child_faces,
    child_peer,
    coarse_faces,
):
    n_dom, n_sub = sizes
    elems = nodal_values.shape[1]
    krons = [np.kron(HALVES[m // 2], HALVES[m % 2]) for m in range(4)]
    mortar = np.concatenate([np.concatenate([m, m.T], axis=1) for m in krons], axis=0)
    held = (elems // 128, NPTS**3, 128)
    side_rows = up(max(sub_faces.shape[1], near_faces.shape[1]))
    small = [
        levels.reshape(1, elems),
        local_faces,
        sub_faces,
        near_faces,
        far_faces,
        child_faces,
        coarse_faces.reshape(1, n_dom),
        jnp.asarray(stencils(), BF16),
        jnp.asarray(mortar, F32),
    ]
    hbm = pl.BlockSpec(memory_space=pltpu.HBM)
    vmem = pl.BlockSpec(memory_space=pltpu.VMEM)
    return pl.pallas_call(
        functools.partial(kernel, sizes),
        out_shape=pltpu.VMEM(nodal_values.shape, F32),
        in_specs=[hbm] * 12,
        out_specs=vmem,
        scratch_shapes=[pltpu.VMEM(item.shape, item.dtype) for item in small]
        + [
            pltpu.SMEM(child_peer.shape, I32),
            pltpu.VMEM(held, F32),
            pltpu.VMEM(held, F32),
            pltpu.VMEM(held, F32),
            pltpu.VMEM(held, F32),
            pltpu.VMEM(held, F32),
            pltpu.VMEM((4, side_rows, 128), F32),
            pltpu.VMEM((4, side_rows, 128), F32),
            pltpu.VMEM((n_dom, 8, 128), F32),
            pltpu.VMEM((n_dom, 8, 128), F32),
            pltpu.SemaphoreType.DMA((len(small) + 1,)),
            pltpu.SemaphoreType.DMA((2, held[0], NPTS**3 // 128)),
            pltpu.SemaphoreType.DMA((4,)),
            pltpu.SemaphoreType.DMA((4,)),
            pltpu.SemaphoreType.DMA((n_dom,)),
            pltpu.SemaphoreType.DMA((n_dom,)),
        ],
        compiler_params=pltpu.CompilerParams(
            collective_id=0, has_side_effects=True, vmem_limit_bytes=60 * 1024 * 1024
        ),
    )(
        nodal_values,
        kappa,
        *small,
        child_peer,
    )


def solution(mesh):
    sizes = (mesh.shape["dom"], mesh.shape["sub"])
    wide = P(None, ("dom", "sub"))
    flat = P(("dom", "sub"))
    in_specs = (wide, wide, flat, wide, wide, wide, wide, wide, flat, flat)
    return jax.shard_map(
        functools.partial(body, sizes),
        mesh=mesh,
        in_specs=in_specs,
        out_specs=wide,
        check_vma=False,
    )
```
